32 devices in a mesh: shot: 16 (over z, x, core), coil: 2 (over y).
Axes of the slice: x: 2, y: 2, z: 4, core: 2. Of those that a mesh axis runs over, the one named last changes fastest.
Arguments:
- image: float32 [2, 2, 320, 320], P('coil', None, 'shot'), may hold values from -6 to 6
- sensitivity: bfloat16 [4, 2, 2, 320, 320], P('coil'), may hold values from -3 to 3
- warp_table: bfloat16 [16, 2, 128, 128], P('shot')
- warp_source: int32 [16, 800, 2], P('shot'), may hold values from 0 to 799
- warp_live: int32 [16, 800, 2], P('shot'), may hold values 0 or 1
- sampled_lines: int32 [16, 20], P('shot'), may hold values from 0 to 319, as said below
- measured: float32 [16, 4, 2, 20, 640], P('shot', 'coil'), may hold values from -6 to 6
Outputs:
- image_out: float32 [2, 2, 320, 320], P('coil', None, 'shot')
- residual_out: float32 [16, 4, 2, 20, 640], P('shot', 'coil')
The draws below stay inside these ranges and needn't reach their ends.
Inputs may be any that keep to these rules, and one draw needn't show every extreme that they name: `sampled_lines`: taken together, the shots acquire each of the 320 phase-encode lines exactly once.
All inputs are finite; a program needn't handle non-finite values. No bound on the sum of `warp_live` on one device may be relied on, other than what follows from the above.
Results may differ from the reference program's by a relative error of at most 0.017.
Values may be sent and summed in bfloat16 or wider, within the bound.
No kernel may reach another device: no remote copies, remote signals or barrier semaphores. Data moves between devices by JAX's collectives and lax.ppermute only.
A program may use at most 128 MiB of HBM per device.

```python
import math
import jax
import jax.numpy as jnp
from jax import lax

NR = 320
NC = 320
BLK = 128
KBLK = 2
STEPS = 1
SHOTS = 16
COILS = 4
NZ = 2
LINES = 20
NB = 800


def draw_sampled_lines(key, part):
    order = jax.random.permutation(key, NR)
    return order.astype(jnp.int32).reshape(SHOTS, LINES)


def draw_warp_source(key, part):
    near_key = jax.random.fold_in(key, 11)
    far_key = jax.random.fold_in(key, 12)
    pick_key = jax.random.fold_in(key, 13)
    offsets = jax.random.randint(near_key, (SHOTS, NB, KBLK), -3, 4)
    blocks = jnp.arange(NB, dtype=jnp.int32)[None, :, None]
    picked = jnp.clip(blocks + offsets, 0, NB - 1).astype(jnp.int32)
    far_blocks = jax.random.randint(far_key, (SHOTS, NB, KBLK), 0, NB).astype(jnp.int32)
    choose = jax.random.randint(pick_key, (SHOTS, NB, KBLK), 0, 8) == 0
    picked = jnp.where(choose, far_blocks, picked).astype(jnp.int32)
    picked = picked.at[:, 0, 0].set(0)
    picked = picked.at[:, NB - 1, 0].set(NB - 1)
    return picked.astype(jnp.int32)


def draw_sensitivity(key, part):
    rows = jnp.arange(NR, dtype=jnp.float32) / (NR - 1)
    rank = jax.random.permutation(jax.random.fold_in(key, 21), COILS).astype(jnp.float32)
    level = rank / max(COILS - 1, 1)
    values = jnp.clip(jax.random.normal(key, (COILS, NZ, 2, NR, NC), jnp.float32), -6.0, 6.0) * 0.5
    factor = 0.5 + rows
    coil_factor = 0.5 + level
    values = values * coil_factor[:, None, None, None, None]
    values = jnp.clip(values * factor[:, None], -3.0, 3.0)
    return values.astype(jnp.bfloat16)


def draw_warp_table(key, part):
    shots = jnp.arange(SHOTS, dtype=jnp.float32) / max(SHOTS - 1, 1)
    base = (BLK * KBLK) ** (-0.5)
    values = jnp.clip(jax.random.normal(key, (SHOTS, KBLK, BLK, BLK), jnp.float32), -6.0, 6.0)
    factor = 0.6 + 1.2 * shots
    values = values * base * factor[:, None, None, None]
    return values.astype(jnp.bfloat16)


def with_ends(drawn, stream_key, least, high):
    longest = drawn.shape.index(max(drawn.shape))
    spots = []
    for shift in (0, 1):
        where = [jax.random.randint(jax.random.fold_in(stream_key, axis), (), 0, length) for axis, length in enumerate(drawn.shape)]
        where[longest] = (where[longest] + shift) % drawn.shape[longest]
        spots.append(tuple(where))
    return drawn.at[spots[0]].set(least).at[spots[1]].set(high)


def levels(rng, extent, pieces, least, largest):
    def one(axis_at, blocks):
        heights = jax.random.uniform(jax.random.fold_in(jax.random.fold_in(rng, 6), axis_at), (blocks,), jnp.float32, least / len(pieces), largest / len(pieces))
        return jnp.repeat(jnp.exp(heights), extent[axis_at] // blocks).reshape((-1,) + (1,) * (len(extent) - axis_at - 1))

    loudness = one(*pieces[0])
    for cut in pieces[1:]:
        loudness = loudness * one(*cut)
    return loudness


def noise(stream_key, extent, scale, most, cuts=(), kind=jnp.bfloat16):
    level = levels(stream_key, extent, cuts, -0.22, 0.18) if cuts else 1.0
    drawn = jax.random.normal(stream_key, extent, jnp.float32) * scale * level
    return jnp.minimum(jnp.maximum(drawn, -most), most).astype(kind)


def setup_inputs(seed: int = 0) -> dict:
    key_list = jax.random.split(jax.random.key(seed), 8)
    return {
        "image": noise(key_list[0], (NZ, 2, NR, NC), 1.0, 6.0, ((0, 2), (2, 16)), jnp.float32),
        "sensitivity": draw_sensitivity(jax.random.fold_in(key_list[7], 71), 0),
        "warp_table": draw_warp_table(jax.random.fold_in(key_list[7], 71), 0),
        "warp_source": draw_warp_source(jax.random.fold_in(key_list[7], 71), 0),
        "warp_live": with_ends((jax.random.randint(key_list[4], (SHOTS, NB, KBLK), 0, 4) < 3).astype(jnp.int32), jax.random.fold_in(key_list[4], 1), 0, 1),
        "sampled_lines": draw_sampled_lines(jax.random.fold_in(key_list[7], 71), 0),
        "measured": noise(key_list[6], (SHOTS, COILS, NZ, LINES, 2 * NC), 1.0, 6.0, ((0, 16), (1, 2)), jnp.float32),
    }


highest = lax.Precision.HIGHEST

def contract(form, left, right):
    return jnp.einsum(form, left.astype(jnp.float32), right.astype(jnp.float32), precision=highest)

def product(left, right):
    return jnp.dot(left.astype(jnp.float32), right.astype(jnp.float32), precision=highest)

def phase_table(line_rows, length):
    positions = jnp.arange(length, dtype=jnp.int32)
    phases = line_rows[:, None] * positions[None, :] % length
    angles = phases.astype(jnp.float32) * (-2.0 * math.pi / length)
    factor = 1.0 / math.sqrt(length)
    real_part = jnp.cos(angles) * factor
    imag_part = jnp.sin(angles) * factor
    upper = jnp.concatenate([real_part, -imag_part], axis=1)
    lower = jnp.concatenate([imag_part, real_part], axis=1)
    return jnp.concatenate([upper, lower], axis=0).astype(jnp.bfloat16)

def apply_warp(volume, kernels, source, live_mask):
    slices = volume.shape[0]
    block_width = kernels.shape[1]
    blocks = volume.reshape(slices, 2, -1, block_width)
    block_count = blocks.shape[2]
    summed = jnp.zeros((slices, 2, block_count, block_width), jnp.float32)
    for member in range(kernels.shape[0]):
        picked = jnp.take(blocks, source[:, member], axis=2)
        shifted = product(picked.reshape(-1, block_width), kernels[member]).reshape(slices, 2, block_count, block_width)
        summed = summed + live_mask[:, member].astype(jnp.float32)[:, None] * shifted
    return summed.reshape(volume.shape)

def warp_adjoint(volume, kernels, source, live_mask):
    slices = volume.shape[0]
    block_width = kernels.shape[1]
    blocks = volume.reshape(slices, 2, -1, block_width)
    block_count = blocks.shape[2]
    summed = jnp.zeros((slices, 2, block_count, block_width), jnp.float32)
    for member in range(kernels.shape[0]):
        spread = product(blocks.reshape(-1, block_width), kernels[member].T).reshape(slices, 2, block_count, block_width)
        spread = live_mask[:, member].astype(jnp.float32)[:, None] * spread
        summed = summed.at[:, :, source[:, member], :].add(spread)
    return summed.reshape(volume.shape)

def coil_forward(warped, sensitivity, section_one, section_two):
    coils, slices, _two, row_count, col_count = sensitivity.shape
    warp_real = warped[:, 0].astype(jnp.float32)
    warp_imag = warped[:, 1].astype(jnp.float32)
    sens_real = sensitivity[:, :, 0].astype(jnp.float32)
    sens_imag = sensitivity[:, :, 1].astype(jnp.float32)
    coil_real = sens_real * warp_real - sens_imag * warp_imag
    coil_imag = sens_real * warp_imag + sens_imag * warp_real
    coil_image = jnp.stack([coil_real, coil_imag], axis=2).astype(jnp.bfloat16)
    stacked = coil_image.reshape(coils, slices, 2 * row_count, col_count)
    phase_rows = contract('ab,czbn->czan', section_one, stacked).astype(jnp.bfloat16)
    line_count = section_one.shape[0] // 2
    regrouped = phase_rows.reshape(coils, slices, 2, line_count, col_count).transpose(0, 1, 3, 2, 4)
    regrouped = regrouped.reshape(coils, slices, line_count, 2 * col_count)
    return contract('czln,nm->czlm', regrouped, section_two)

def coil_adjoint(residual, sensitivity, section_one, section_two):
    coils, slices, _two, row_count, col_count = sensitivity.shape
    line_count = residual.shape[2]
    back_two = contract('czlm,nm->czln', residual.astype(jnp.bfloat16), section_two).astype(jnp.bfloat16)
    regrouped = back_two.reshape(coils, slices, line_count, 2, col_count).transpose(0, 1, 3, 2, 4)
    regrouped = regrouped.reshape(coils, slices, 2 * line_count, col_count)
    back = contract('ab,czan->czbn', section_one, regrouped).reshape(coils, slices, 2, row_count, col_count)
    sens_real = sensitivity[:, :, 0].astype(jnp.float32)
    sens_imag = sensitivity[:, :, 1].astype(jnp.float32)
    comb_real = lax.optimization_barrier(jnp.sum(sens_real * back[:, :, 0] + sens_imag * back[:, :, 1], axis=0))
    comb_imag = lax.optimization_barrier(jnp.sum(sens_real * back[:, :, 1] - sens_imag * back[:, :, 0], axis=0))
    return jnp.stack([comb_real, comb_imag], axis=1)

def readout_table():
    return phase_table(jnp.arange(NC, dtype=jnp.int32), NC).T

def forward_all(volume, sensitivity, warp_table, warp_source, warp_live, sampled_lines):
    section_two = readout_table()

    def one_shot(items):
        kernels, source, live_mask, line_rows = items
        warped = apply_warp(volume, kernels, source, live_mask).astype(jnp.bfloat16)
        return coil_forward(warped, sensitivity, phase_table(line_rows, NR), section_two)
    return lax.map(one_shot, (warp_table, warp_source, warp_live, sampled_lines))

def adjoint_all(residual, sensitivity, warp_table, warp_source, warp_live, sampled_lines):
    section_two = readout_table()

    def one_shot(summed, items):
        kernels, source, live_mask, line_rows, shot_residual = items
        combined = coil_adjoint(shot_residual, sensitivity, phase_table(line_rows, NR), section_two)
        combined = combined.astype(jnp.bfloat16)
        return (summed + warp_adjoint(combined, kernels, source, live_mask), None)
    start = jnp.zeros((NZ, 2, NR, NC), jnp.float32)
    return lax.scan(one_shot, start, (warp_table, warp_source, warp_live, sampled_lines, residual))[0]

def reference(image, sensitivity, warp_table, warp_source, warp_live, sampled_lines, measured):
    shared = (sensitivity, warp_table, warp_source, warp_live, sampled_lines)
    residual = forward_all(image.astype(jnp.bfloat16), *shared) - measured
    for iteration in range(STEPS):
        gradient = adjoint_all(residual, *shared)
        image_of_grad = forward_all(gradient.astype(jnp.bfloat16), *shared)
        grad_norm = jnp.sum(gradient * gradient)
        image_norm = jnp.sum(image_of_grad * image_of_grad)
        step_size = grad_norm / (image_norm + 1e-06)
        image = image - step_size * gradient
        residual = residual - step_size * image_of_grad
    return (image, residual)
```

```python
import functools
import math

import jax
import jax.numpy as jnp
import numpy as np
from jax import lax
from jax.experimental import pallas as pl
from jax.experimental.pallas import tpu as pltpu
from jax.sharding import PartitionSpec as P

BF = jnp.bfloat16
F32 = jnp.float32
AXES = ("shot", "coil")


def round_up(value, unit):
    return -(-value // unit) * unit


def dft_tables(rows, cols):
    def parts(length):
        index = np.arange(length, dtype=np.int64)
        angle = (index[:, None] * index[None, :] % length) * (-2.0 * math.pi / length)
        return np.cos(angle) / math.sqrt(length), np.sin(angle) / math.sqrt(length)

    real, imag = parts(cols)
    readout = np.block([[real, imag], [-imag, real]])
    real, imag = parts(rows)
    lines = []
    for odd in (0, 1):
        re, im = real[:, odd::2], imag[:, odd::2]
        lines.append(np.concatenate([re, -im], axis=1))
        lines.append(np.concatenate([im, re], axis=1))
    as_bf = lambda t: t.astype(np.float32).astype(jnp.bfloat16)
    return as_bf(readout), as_bf(np.stack(lines))


def dot(left, right):
    return jnp.dot(left, right, preferred_element_type=F32)


def dot_nt(left, right):
    return lax.dot_general(left, right, (((1,), (1,)), ((), ())), preferred_element_type=F32)


def call(body, out_shape, scratch=(), smem=0, name=None):
    def run(*args):
        specs = [pl.BlockSpec(memory_space=pltpu.SMEM)] * smem
        specs += [pl.BlockSpec(memory_space=pltpu.VMEM)] * (len(args) - smem)
        return pl.pallas_call(
            body,
            out_shape=out_shape,
            in_specs=specs,
            out_specs=jax.tree.map(lambda _: pl.BlockSpec(memory_space=pltpu.VMEM), out_shape),
            scratch_shapes=list(scratch),
            compiler_params=pltpu.CompilerParams(vmem_limit_bytes=56 * 1024 * 1024),
            name=name,
        )(*args)

    return run


def select_body(by_row, by_col, pick, spread):
    members, blocks, _ = pick.shape
    along = lax.broadcasted_iota(jnp.int32, (blocks, blocks), 1)
    down = lax.broadcasted_iota(jnp.int32, (blocks, blocks), 0)
    for k in range(members):
        pick[k] = jnp.where(along == by_row[:, k : k + 1], 1.0, 0.0).astype(BF)
        spread[k] = jnp.where(down == by_col[k : k + 1, :], 1.0, 0.0).astype(BF)


def lines_body(lines, tables, rows_out, cols_out):
    lp = rows_out.shape[0] // 4
    count = tables.shape[1]
    size = tables.shape[2]
    chosen = lines[...] == lax.broadcasted_iota(jnp.int32, (lp, count), 1)
    chosen = jnp.where(chosen, 1.0, 0.0).astype(BF)
    for part in range(4):
        rows_out[part * lp : (part + 1) * lp, :] = dot(chosen, tables[part]).astype(BF)
    eye = lax.broadcasted_iota(jnp.int32, (size, size), 0) == lax.broadcasted_iota(
        jnp.int32, (size, size), 1
    )
    eye = jnp.where(eye, 1.0, 0.0).astype(BF)
    cols_out[...] = dot_nt(eye, rows_out[...]).astype(BF)


def pair_body(maps, out):
    count, rows, cols = maps.shape
    half = rows // 2
    at = lax.broadcasted_iota(jnp.int32, (rows, rows), 0)
    want = jnp.where(at < half, 2 * at, 2 * (at - half) + 1)
    order = jnp.where(lax.broadcasted_iota(jnp.int32, (rows, rows), 1) == want, 1.0, 0.0).astype(BF)
    lane = lax.broadcasted_iota(jnp.int32, (cols, 2 * cols), 1)
    twice = lax.broadcasted_iota(jnp.int32, (cols, 2 * cols), 0) == jnp.where(
        lane < cols, lane, lane - cols
    )
    twice = jnp.where(twice, 1.0, 0.0).astype(BF)
    low = lax.broadcasted_iota(jnp.int32, (half, 2 * cols), 1) < cols
    for i in range(count):
        sorted_rows = dot(order, maps[i]).astype(BF)
        wide = dot(sorted_rows, twice)
        out[i] = jnp.where(low, wide[:half], wide[half:]).astype(BF)


def warp(volume, pick, kernels, width):
    members = pick.shape[0]
    picked = [dot(pick[k], volume).astype(BF) for k in range(members)]
    table = jnp.concatenate([kernels[k] for k in range(members)], axis=0)
    planes = []
    for plane in range(2):
        cut = slice(plane * width, (plane + 1) * width)
        planes.append(dot(jnp.concatenate([p[:, cut] for p in picked], axis=1), table).astype(BF))
    return planes


def pairs_of(ref, plane, rows, width, tiles):
    return jnp.concatenate([ref[plane, pl.ds(j, rows, stride=tiles), :] for j in range(tiles)], axis=1)


def coil_rows(warped, sens, rows_table, z, coils, slices, width, lines_out):
    half, wide = sens.shape[1], sens.shape[2]
    cols = wide // 2
    tiles = wide // width
    lp = rows_table.shape[0] // 4
    real = pairs_of(warped, 2 * z, half, width, tiles)
    imag = pairs_of(warped, 2 * z + 1, half, width, tiles)
    low = lax.broadcasted_iota(jnp.int32, (lp, wide), 1) < cols
    for c in range(coils):
        at = (c * slices + z) * 2
        sr, si = sens[at].astype(F32), sens[at + 1].astype(F32)
        coil = jnp.concatenate([sr * real - si * imag, sr * imag + si * real], axis=0).astype(BF)
        found = dot(rows_table[...], coil)
        stay = jnp.where(low, found[:lp], found[3 * lp :])
        move = jnp.where(low, found[lp : 2 * lp], found[2 * lp : 3 * lp])
        where = (c * slices + z) * lp
        lines_out[where : where + lp, :] = (stay + pltpu.roll(move, cols, 1)).astype(BF)


def plane_at(slots, position, planes):
    half = planes // 2
    return position ^ slots[0] if position < half else (position - half) ^ slots[2]


def first_body(
    slots, mine_ref, other_ref, pick, spread, kernels, sens, rows_table, cols_table, readout, measured,
    residual, send, keep, volume, warped, lines, *, slab, coils, slices, shots, coil_parts,
):
    blocks, width = warped.shape[1], warped.shape[2]
    members = pick.shape[0]
    half, wide = sens.shape[1], sens.shape[2]
    cols = wide // 2
    tiles = wide // width
    lp = rows_table.shape[0] // 4
    count = measured.shape[1]
    per_part = slices // coil_parts
    own = mine_ref.shape[0]
    for z in range(slices):
        part, inner = z // per_part, z % per_part
        for s in range(shots):
            slot = slots[6 + s * coil_parts + part]
            source = jnp.where(slot < own, slot, 0)
            far = jnp.where(slot < own, 0, slot - own)
            piece = jnp.where(slot < own, mine_ref[source].astype(F32), other_ref[far].astype(F32))
            for plane in range(2):
                start = (inner * 2 + plane) * slab
                volume[s * slab : (s + 1) * slab, plane * width : (plane + 1) * width] = piece[
                    start : start + slab
                ]
        planes = warp(volume[...].astype(BF), pick, kernels, width)
        for plane in range(2):
            warped[2 * z + plane] = planes[plane].astype(F32)
        coil_rows(warped, sens, rows_table, z, coils, slices, width, lines)
    spectrum = dot(lines[...], readout[...])
    for i in range(coils * slices):
        rows = spectrum[i * lp : i * lp + lp]
        left = rows[:count] - measured[i]
        residual[i] = left
        if count < lp:
            left = jnp.concatenate([left, jnp.zeros((lp - count, wide), F32)], axis=0)
        lines[i * lp : (i + 1) * lp, :] = left.astype(BF)
    back = dot_nt(lines[...], readout[...])
    low = lax.broadcasted_iota(jnp.int32, (lp, wide), 1) < cols
    zero = jnp.zeros((lp, wide), F32)
    for z in range(slices):
        real = jnp.zeros((half, wide), F32)
        imag = jnp.zeros((half, wide), F32)
        for c in range(coils):
            i = c * slices + z
            rows = back[i * lp : (i + 1) * lp]
            turned = pltpu.roll(rows, cols, 1)
            spreadout = jnp.concatenate(
                [
                    jnp.where(low, rows, zero),
                    jnp.where(low, turned, zero),
                    jnp.where(low, zero, turned),
                    jnp.where(low, zero, rows),
                ],
                axis=0,
            ).astype(BF)
            got = dot(cols_table[...], spreadout)
            gr, gi = got[:half], got[half:]
            sr, si = sens[2 * i].astype(F32), sens[2 * i + 1].astype(F32)
            real = real + (sr * gr + si * gi)
            imag = imag + (sr * gi - si * gr)
        for j in range(tiles):
            cut = slice(j * width, (j + 1) * width)
            warped[2 * z, pl.ds(j, half, stride=tiles), :] = real[:, cut]
            warped[2 * z + 1, pl.ds(j, half, stride=tiles), :] = imag[:, cut]
    planes = 2 * slices
    rows_half = blocks // 2
    for pair in range(slices):
        total = jnp.zeros((blocks, 2 * width), F32)
        chosen = [warped[plane_at(slots, 2 * pair + e, planes)].astype(BF) for e in range(2)]
        for k in range(members):
            moved = jnp.concatenate([dot_nt(c, kernels[k]) for c in chosen], axis=1).astype(BF)
            total = total + dot(spread[k], moved)
        total = total.astype(BF)
        for e in range(2):
            at = 2 * pair + e
            target, turn = (keep, slots[1]) if at < planes // 2 else (send, slots[3])
            for h in range(2):
                target[at % (planes // 2), h ^ turn] = total[
                    h * rows_half : (h + 1) * rows_half, e * width : (e + 1) * width
                ]


def second_body(
    slots, near, far, pick, kernels, sens, rows_table, readout, spectrum, sums, norm, own_slab,
    volume, warped, lines, bands, *, slab, coils, slices, shots, coil_parts,
):
    blocks, width = warped.shape[1], warped.shape[2]
    wide = sens.shape[2]
    lp = rows_table.shape[0] // 4
    count = spectrum.shape[1]
    planes = 2 * slices
    rows_half = blocks // 2
    shot, coil = slots[4], slots[5]
    slab_rows = bands.shape[1]
    at_row = lax.broadcasted_iota(jnp.int32, (slab_rows, blocks), 0) + shot * slab
    mine = jnp.where(lax.broadcasted_iota(jnp.int32, (slab_rows, blocks), 1) == at_row, 1.0, 0.0).astype(BF)
    square = jnp.zeros((8, 2 * width), F32)
    for pair in range(slices):
        for e in range(2):
            at = 2 * pair + e
            source, turn = (near, slots[1]) if at < planes // 2 else (far, slots[3])
            for h in range(2):
                volume[h * rows_half : (h + 1) * rows_half, e * width : (e + 1) * width] = source[
                    at % (planes // 2), h ^ turn
                ]
        value = volume[...]
        as_f32 = value.astype(F32)
        square = square + jnp.sum((as_f32 * as_f32).reshape(blocks // 8, 8, 2 * width), axis=0)
        band = dot(mine, value)
        got = warp(value, pick, kernels, width)
        for e in range(2):
            plane = plane_at(slots, 2 * pair + e, planes)
            warped[plane] = got[e].astype(F32)
            bands[plane] = band[:, e * width : (e + 1) * width]
    for z in range(slices):
        coil_rows(warped, sens, rows_table, z, coils, slices, width, lines)
    found = dot(lines[...], readout[...])
    sums[...] = jnp.broadcast_to(jnp.sum(found * found), sums.shape)
    norm[...] = jnp.broadcast_to(jnp.sum(square), norm.shape)
    for i in range(coils * slices):
        spectrum[i] = found[i * lp : i * lp + count]
    own = own_slab.shape[0]
    for i in range(own):
        own_slab[i] = bands[coil * own + i][:slab]


def exchange_pairs(partner, shots, coils):
    pairs = []
    for s in range(shots):
        for c in range(coils):
            t, d = partner(s, c)
            pairs.append((s * coils + c, t * coils + d))
    return pairs


def shards(shots, coil_parts, image, sensitivity, warp_table, warp_source, warp_live, sampled_lines, measured):
    coils, slices, _, rows, cols = sensitivity.shape
    members, width = warp_table.shape[1], warp_table.shape[2]
    blocks = warp_source.shape[1]
    count = sampled_lines.shape[1]
    lp = round_up(count, 16)
    own_slices = image.shape[0]
    slab = blocks // shots
    planes = 2 * slices
    shot, coil = lax.axis_index("shot"), lax.axis_index("coil")

    core = lambda s, c: (s ^ 1, c)
    by_shot = lambda s, c: (s ^ 2, c)
    by_coil = lambda s, c: (s, c ^ 1)
    first_way = lambda s, c: by_coil(s, c) if s & 1 == 0 else by_shot(s, c)
    second_way = lambda s, c: by_shot(s, c) if s & 1 == 0 else by_coil(s, c)
    rest = [lambda s, c, b=b: (s ^ b, c) for b in (1 << i for i in range(2, shots.bit_length() - 1))]
    rest += [lambda s, c, b=b: (s, c ^ b) for b in (1 << i for i in range(1, coil_parts.bit_length() - 1))]

    def swap(value, partner):
        return lax.ppermute(value, AXES, exchange_pairs(partner, shots, coil_parts))

    piece = image.astype(BF).reshape(1, own_slices * 2 * slab, width)
    steps = list(reversed(rest)) + [second_way, first_way]
    for partner in steps:
        piece = jnp.concatenate([piece, swap(piece, partner)], axis=0)
    other = swap(piece, core)

    s_of = jnp.arange(shots, dtype=jnp.int32)[:, None]
    c_of = jnp.arange(coil_parts, dtype=jnp.int32)[None, :]
    ds, dc = s_of ^ shot, c_of ^ coil
    even = (s_of & 1) == 0
    one, two = (ds >> 1) & 1, dc & 1
    slot = jnp.zeros((shots, coil_parts), jnp.int32)
    weight = 1
    shot_bits = shots.bit_length() - 1
    coil_bits = coil_parts.bit_length() - 1
    rest_values = [(ds >> i) & 1 for i in range(2, shot_bits)] + [(dc >> i) & 1 for i in range(1, coil_bits)]
    for value in reversed(rest_values):
        slot = slot + weight * value
        weight *= 2
    slot = slot + weight * jnp.where(even, one, two)
    weight *= 2
    slot = slot + weight * jnp.where(even, two, one)
    weight *= 2
    slot = slot + weight * (ds & 1)
    my_even = (shot & 1) == 0
    bit_a = jnp.where(my_even, coil & 1, (shot >> 1) & 1)
    bit_b = jnp.where(my_even, (shot >> 1) & 1, coil & 1)
    flip = (shot & 1) * (planes // 2) + bit_a * (planes // 4)
    far_flip = (1 - (shot & 1)) * (planes // 2) + bit_b * (planes // 4)
    order = jnp.stack([flip, bit_b, far_flip, bit_a, shot, coil]).astype(jnp.int32)
    slots = jnp.concatenate([order, slot.reshape(-1)])

    readout_np, lines_np = dft_tables(rows, cols)
    readout, line_tables = jnp.asarray(readout_np), jnp.asarray(lines_np)
    kernels = warp_table[0]
    source = jnp.where(warp_live[0] != 0, warp_source[0], -1)
    shape = jax.ShapeDtypeStruct
    pick, spread = call(select_body, [shape((members, blocks, blocks), BF)] * 2, name="select")(
        source, source.T
    )
    lines = jnp.pad(sampled_lines[0], (0, lp - count), constant_values=-1)[:, None]
    rows_table, cols_table = call(
        lines_body, [shape((4 * lp, rows), BF), shape((rows, 4 * lp), BF)], name="lines"
    )(lines, line_tables)
    maps = coils * slices * 2
    sens = call(pair_body, shape((maps, rows // 2, 2 * cols), BF), name="pairs")(
        sensitivity.reshape(maps, rows, cols)
    )
    sizes = dict(slab=slab, coils=coils, slices=slices, shots=shots, coil_parts=coil_parts)
    batch = coils * slices
    residual, send, keep = call(
        functools.partial(first_body, **sizes),
        [shape((batch, count, 2 * cols), F32)] + [shape((planes // 2, 2, blocks // 2, width), BF)] * 2,
        scratch=[
            pltpu.VMEM((blocks, 2 * width), F32),
            pltpu.VMEM((planes, blocks, width), F32),
            pltpu.VMEM((batch * lp, 2 * cols), BF),
        ],
        smem=1,
        name="first",
    )(
        slots, piece, other, pick, spread, kernels, sens, rows_table, cols_table, readout,
        measured.reshape(batch, count, 2 * cols),
    )

    def add(left, right):
        return (left.astype(F32) + right.astype(F32)).astype(BF)

    got = swap(send, core)
    quarter = planes // 4
    out2, stay2 = add(keep[quarter:], got[quarter:]), add(keep[:quarter], got[:quarter])
    got = swap(out2, first_way)
    out3, total = add(stay2[:, 1], got[:, 1]), add(stay2[:, 0], got[:, 0])
    got = swap(out3, second_way)
    total = add(total, got)
    for partner in rest:
        total = add(total, swap(total, partner))
    both = jnp.stack([total, swap(total, second_way)], axis=1)
    near = jnp.concatenate([both, swap(both, first_way)], axis=0)
    far = swap(near, core)

    devices = shots * coil_parts
    spectrum, sums, norm, own = call(
        functools.partial(second_body, **sizes),
        [
            shape((batch, count, 2 * cols), F32),
            shape((devices, 128), F32),
            shape((1, 128), F32),
            shape((own_slices * 2, slab, width), F32),
        ],
        scratch=[
            pltpu.VMEM((blocks, 2 * width), BF),
            pltpu.VMEM((planes, blocks, width), F32),
            pltpu.VMEM((batch * lp, 2 * cols), BF),
            pltpu.VMEM((planes, round_up(slab, 16), width), F32),
        ],
        smem=1,
        name="second",
    )(slots, near, far, pick, kernels, sens, rows_table, readout)
    image_norm = jnp.sum(lax.all_to_all(sums, AXES, 0, 0, tiled=True)[:, 0])
    step_size = norm[0, 0] / (image_norm + 1e-06)
    image = image - step_size * own.reshape(image.shape)
    residual = (residual - step_size * spectrum).reshape(measured.shape)
    return image, residual


def solution(mesh):
    body = functools.partial(shards, mesh.shape["shot"], mesh.shape["coil"])
    return jax.shard_map(
        body,
        mesh=mesh,
        in_specs=(
            P("coil", None, "shot", None),
            P("coil", None, None, None, None),
            P("shot", None, None, None),
            P("shot", None, None),
            P("shot", None, None),
            P("shot", None),
            P("shot", "coil", None, None, None),
        ),
        out_specs=(P("coil", None, "shot", None), P("shot", "coil", None, None, None)),
        check_vma=False,
    )
```

```python
import functools
import math

import jax
import jax.numpy as jnp
import numpy as np
from jax import lax
from jax.experimental import pallas as pl
from jax.experimental.pallas import tpu as pltpu
from jax.sharding import PartitionSpec as P


BF = jnp.bfloat16
F32 = jnp.float32
AXES = ("shot", "coil")


def round_up(value, unit):
    return -(-value // unit) * unit


def dft_tables(rows, cols):
    def parts(length):
        index = np.arange(length, dtype=np.int64)
        angle = (index[:, None] * index[None, :] % length) * (-2.0 * math.pi / length)
        return np.cos(angle) / math.sqrt(length), np.sin(angle) / math.sqrt(length)

    real, imag = parts(cols)
    readout = np.block([[real, imag], [-imag, real]])
    real, imag = parts(rows)
    lines = []
    for odd in (0, 1):
        re, im = real[:, odd::2], imag[:, odd::2]
        lines.append(np.concatenate([re, -im], axis=1).T)
        lines.append(np.concatenate([im, re], axis=1).T)
    as_bf = lambda t: t.astype(np.float32).astype(jnp.bfloat16)
    return as_bf(readout), as_bf(np.stack(lines))


def dot(left, right):
    return jnp.dot(left, right, preferred_element_type=F32)


def dot_nt(left, right):
    return lax.dot_general(left, right, (((1,), (1,)), ((), ())), preferred_element_type=F32)


def call(body, out_shape, slices, scratch=(), smem=0, far=0):
    def run(*args):
        near = len(args) - smem - far
        specs = [pl.BlockSpec(memory_space=pltpu.SMEM)] * smem
        specs += [pl.BlockSpec(memory_space=pltpu.VMEM)] * near
        specs += [pl.BlockSpec(memory_space=pl.ANY)] * far
        args = list(args[: smem + near]) + [
            pltpu.with_memory_space_constraint(arg, pltpu.HBM) for arg in args[smem + near :]
        ]
        return pl.pallas_call(
            body,
            out_shape=out_shape,
            in_specs=specs,
            out_specs=jax.tree.map(lambda _: pl.BlockSpec(memory_space=pltpu.VMEM), out_shape),
            scratch_shapes=list(scratch),
            compiler_params=pltpu.CompilerParams(
                vmem_limit_bytes=min(8 + 6 * slices, 56) * 1024 * 1024
            ),
        )(*args)

    return run


def fetch(pairs, sems):
    copies = [pltpu.make_async_copy(a, b, sems.at[i]) for i, (a, b) in enumerate(pairs)]
    for copy in copies:
        copy.start()
    return copies


def wanted_of(source_far, live_far, source, live, sems):
    for copy in fetch([(source_far, source), (live_far, live)], sems):
        copy.wait()
    return jnp.where(live[...] != 0, source[...], -1)


def spread_body(slots, source_far, live_far, spread, source, live, wanted, sems):
    blocks, wide = spread.shape
    table = wanted_of(source_far, live_far, source, live, sems)
    for k in range(wide // blocks):
        wanted[:, k * blocks : (k + 1) * blocks] = table[k : k + 1, :]
    down = lax.broadcasted_iota(jnp.int32, (blocks, wide), 0)
    spread[...] = jnp.where(down == jnp.broadcast_to(wanted[...], (blocks, wide)), 1.0, 0.0).astype(BF)


def pick_body(slots, source_far, live_far, pick, source, live, sems):
    members, blocks, _ = pick.shape
    table = wanted_of(source_far, live_far, source, live, sems)
    full = round_up(blocks, 128)
    along = lax.broadcasted_iota(jnp.int32, (blocks, blocks), 1).astype(F32)
    for k in range(members):
        flat = jnp.broadcast_to(table[k : k + 1, :], (8, blocks)).astype(F32)
        if full > blocks:
            flat = jnp.concatenate([flat, jnp.zeros((8, full - blocks), F32)], axis=1)
        by_row = flat.T[:blocks, :1]
        pick[k] = jnp.where(along == by_row, 1.0, 0.0).astype(BF)


def tables_body(*refs, coils, kept):
    maps_far, lines_far, line_tables_far, *refs = refs
    kept_far, refs = refs[:kept], refs[kept:]
    rows_out, cols_out, *refs = refs
    sens, kept_out, refs = refs[:coils], refs[coils : coils + kept], refs[coils + kept :]
    maps, lines, line_tables, padded, wide, sems = refs
    first, second, third, *rest = fetch(
        [(maps_far, maps), (line_tables_far, line_tables), (lines_far, lines), *zip(kept_far, kept_out)],
        sems,
    )
    first.wait()
    for c in range(coils):
        pair_body(maps, c, sens[c], wide)
    second.wait()
    third.wait()
    lines_body(lines, line_tables, rows_out, cols_out, padded)
    for copy in rest:
        copy.wait()


def lines_body(lines, tables, rows_out, cols_out, padded):
    lp = rows_out.shape[0] // 4
    count = tables.shape[2]
    padded[...] = jnp.full(padded.shape, -1, jnp.int32)
    padded[:, : lines.shape[1]] = lines[...]
    wide = jnp.broadcast_to(padded[:, :lp], (count, lp))
    chosen = jnp.where(lax.broadcasted_iota(jnp.int32, (count, lp), 0) == wide, 1.0, 0.0).astype(BF)
    eye = lax.broadcasted_iota(jnp.int32, (lp, lp), 0) == lax.broadcasted_iota(jnp.int32, (lp, lp), 1)
    eye = jnp.where(eye, 1.0, 0.0).astype(BF)
    for part in range(4):
        got = dot(tables[part], chosen).astype(BF)
        cols_out[:, part * lp : (part + 1) * lp] = got
        rows_out[part * lp : (part + 1) * lp, :] = dot_nt(eye, got).astype(BF)


def pair_body(maps, coil, out, wide):
    count, rows, cols = maps.shape[1:]
    half = rows // 2
    low = lax.broadcasted_iota(jnp.int32, (half, 2 * cols), 1) < cols
    width = wide.shape[2]
    used = range(0, cols, width)
    spare = [jnp.zeros((half, 2 * cols - width * len(used)), F32)]
    for i in range(count):
        for t, start in enumerate(used):
            stop = min(start + width, cols)
            wide[t, :, : stop - start] = maps[coil, i, :, start:stop].astype(F32)
        even, odd = (
            jnp.concatenate([wide[t, pl.ds(e, half, stride=2), :] for t in range(len(used))] + spare, axis=1)
            for e in range(2)
        )
        out[i] = jnp.where(low, even, pltpu.roll(odd, cols, 1)).astype(BF)


def halves_dot(left, right):
    half = left.shape[0] // 2
    return jnp.concatenate([dot(left[:half, :], right), dot(left[half:, :], right)], axis=0)


def warp(volume, pick, kernels, width):
    members = kernels.shape[0]
    picked = [dot(pick[k], volume).astype(BF) for k in range(members)]
    table = jnp.concatenate([kernels[k] for k in range(members)], axis=0)
    planes = []
    for e in range(2):
        cut = slice(e * width, (e + 1) * width)
        planes.append(dot(jnp.concatenate([p[:, cut] for p in picked], axis=1), table))
    return jnp.concatenate(planes, axis=1)


def unwarp(planes, spread, kernels):
    members = kernels.shape[0]
    rows = [
        jnp.concatenate([dot_nt(plane, kernels[k]) for plane in planes], axis=1).astype(BF)
        for k in range(members)
    ]
    return halves_dot(spread, jnp.concatenate(rows, axis=0)).astype(BF)


def pairs_of(ref, plane, rows, tiles):
    return jnp.concatenate([ref[plane, pl.ds(j, rows, stride=tiles), :] for j in range(tiles)], axis=1)


def coil_rows(warped, at, sens, z, rows_table, place, lines):
    width = warped.shape[2]
    half, wide = sens[0].shape[1], sens[0].shape[2]
    cols = wide // 2
    tiles = wide // width
    lp = rows_table.shape[0] // 4
    real = pairs_of(warped, at, half, tiles).astype(BF)
    imag = pairs_of(warped, at + 1, half, tiles).astype(BF)
    low = lax.broadcasted_iota(jnp.int32, (lp, wide), 1) < cols
    for c, maps in enumerate(sens):
        sr, si = maps[2 * z], maps[2 * z + 1]
        coil = jnp.concatenate([sr * real - si * imag, sr * imag + si * real], axis=0)
        found = dot(rows_table[...], coil)
        stay = jnp.where(low, found[:lp], found[3 * lp :])
        move = jnp.where(low, found[lp : 2 * lp], found[2 * lp : 3 * lp])
        lines[place(c)] = (stay + pltpu.roll(move, cols, 1)).astype(BF)


def readout_of(lines, readout):
    batch, lp, wide = lines.shape
    return dot(lines[...].reshape(batch * lp, wide), readout[...])


def plane_at(slots, position, planes):
    half = planes // 2
    return position ^ slots[0] if position < half else (position - half) ^ slots[2]


def put_halves(target, at, turn, planes):
    rows, width = planes.shape[0] // 2, planes.shape[1] // 2
    for e in range(2):
        for h in range(2):
            target[at + e, h ^ turn] = planes[h * rows : (h + 1) * rows, e * width : (e + 1) * width]


def first_body(slots, mine, other, pick, spread, kernels, *refs, slab, coils, slices, shots, coil_parts):
    sens, refs = refs[:coils], refs[coils:]
    rows_table, cols_table, readout, measured, residual, send, rest, pieces, volume, warped, lines = refs
    width = warped.shape[2]
    half, wide = sens[0].shape[1], sens[0].shape[2]
    cols = wide // 2
    tiles = wide // width
    lp = rows_table.shape[0] // 4
    count = measured.shape[1]
    per_part = slices // coil_parts
    own = mine.shape[0]
    pieces[:own] = mine[...]
    pieces[own:] = other[...]
    for z in range(slices):
        part, inner = z // per_part, z % per_part
        for s in range(shots):
            piece = pieces[slots[6 + s * coil_parts + part]].astype(F32)
            for plane in range(2):
                start = (inner * 2 + plane) * slab
                volume[z, s * slab : (s + 1) * slab, plane * width : (plane + 1) * width] = piece[
                    start : start + slab
                ]
        moved = warp(volume[z].astype(BF), pick, kernels, width)
        for plane in range(2):
            moved_plane = moved[:, plane * width : (plane + 1) * width]
            warped[2 * z + plane] = moved_plane.astype(BF).astype(F32)
        coil_rows(warped, 2 * z, sens, z, rows_table, lambda c, z=z: c * slices + z, lines)
    spectrum = readout_of(lines, readout)
    for c in range(coils):
        for z in range(slices):
            i = c * slices + z
            left = spectrum[i * lp : i * lp + count] - measured[c, :, z, :]
            residual[c, :, z, :] = left
            if count < lp:
                left = jnp.concatenate([left, jnp.zeros((lp - count, wide), F32)], axis=0)
            lines[i] = left.astype(BF)
    back = dot_nt(lines[...].reshape(coils * slices * lp, wide), readout[...])
    low = lax.broadcasted_iota(jnp.int32, (lp, wide), 1) < cols
    zero = jnp.zeros((lp, wide), F32)
    for z in range(slices):
        real, imag = None, None
        for c in range(coils):
            i = c * slices + z
            rows = back[i * lp : (i + 1) * lp]
            turned = pltpu.roll(rows, cols, 1)
            spreadout = jnp.concatenate(
                [
                    jnp.where(low, rows, zero),
                    jnp.where(low, turned, zero),
                    jnp.where(low, zero, turned),
                    jnp.where(low, zero, rows),
                ],
                axis=0,
            ).astype(BF)
            got = dot(cols_table[...], spreadout).astype(BF)
            gr, gi = got[:half], got[half:]
            sr, si = sens[c][2 * z], sens[c][2 * z + 1]
            more_real, more_imag = sr * gr + si * gi, sr * gi - si * gr
            real = more_real if real is None else real + more_real
            imag = more_imag if imag is None else imag + more_imag
        for j in range(tiles):
            cut = slice(j * width, (j + 1) * width)
            warped[2 * z, pl.ds(j, half, stride=tiles), :] = real[:, cut].astype(F32)
            warped[2 * z + 1, pl.ds(j, half, stride=tiles), :] = imag[:, cut].astype(F32)
    planes = 2 * slices
    for at in range(0, planes // 2, 2):
        chosen = [warped[plane_at(slots, planes // 2 + at + e, planes)].astype(BF) for e in range(2)]
        put_halves(send, at, slots[3], unwarp(chosen, spread, kernels))
    for at in range(planes // 2):
        rest[at] = warped[plane_at(slots, at, planes)].astype(BF)


def keep_body(slots, rest, spread, kernels, keep):
    for at in range(0, rest.shape[0], 2):
        put_halves(keep, at, slots[1], unwarp([rest[at], rest[at + 1]], spread, kernels))


def forward_part(slots, start, source, pick, kernels, sens, rows_table, lines, bands, volume, warped, *, slab):
    half_planes = source.shape[0]
    planes = 2 * half_planes
    blocks, width = warped.shape[1], warped.shape[2]
    rows = blocks // 2
    turn = slots[1] if start == 0 else slots[3]
    slab_rows = bands.shape[1]
    at_row = lax.broadcasted_iota(jnp.int32, (slab_rows, blocks), 0) + slots[4] * slab
    mine = jnp.where(lax.broadcasted_iota(jnp.int32, (slab_rows, blocks), 1) == at_row, 1.0, 0.0).astype(BF)
    square = jnp.zeros((8, 2 * width), F32)
    for at in range(0, half_planes, 2):
        for e in range(2):
            for h in range(2):
                volume[h * rows : (h + 1) * rows, e * width : (e + 1) * width] = source[at + e, h ^ turn]
        value = volume[...]
        as_f32 = value.astype(F32)
        square = square + jnp.sum((as_f32 * as_f32).reshape(blocks // 8, 8, 2 * width), axis=0)
        band = dot(mine, value)
        moved = warp(value, pick, kernels, width)
        for e in range(2):
            plane = plane_at(slots, start + at + e, planes)
            cut = slice(e * width, (e + 1) * width)
            warped[plane & 1] = moved[:, cut].astype(BF).astype(F32)
            bands[at + e] = band[:, cut]
        z = plane_at(slots, start + at, planes) >> 1
        coil_rows(warped, 0, sens, z, rows_table, lambda c, at=at: c * (half_planes // 2) + at // 2, lines)
    return square


def near_body(slots, near, pick, kernels, *refs, slab, coils):
    sens, refs = refs[:coils], refs[coils:]
    rows_table, lines, bands, square, volume, warped = refs
    square[...] = forward_part(
        slots, 0, near, pick, kernels, sens, rows_table, lines, bands, volume, warped, slab=slab
    )


def second_body(slots, far, near_lines, near_bands, near_square, pick, kernels, *refs, slab, coils):
    sens, refs = refs[:coils], refs[coils:]
    rows_table, readout, spectrum, sums, norm, own_rows, *refs = refs
    volume, warped, far_lines, far_bands, lines, bands = refs
    half_planes = far.shape[0]
    planes = 2 * half_planes
    slices = half_planes
    width = warped.shape[2]
    wide = sens[0].shape[2]
    cols = wide // 2
    tiles = wide // width
    lp = rows_table.shape[0] // 4
    count = spectrum.shape[1]
    coil = slots[5]
    square = near_square[...] + forward_part(
        slots, half_planes, far, pick, kernels, sens, rows_table, far_lines, far_bands, volume, warped,
        slab=slab,
    )
    for start, some_lines, some_bands in ((0, near_lines, near_bands), (half_planes, far_lines, far_bands)):
        for at in range(half_planes):
            bands[plane_at(slots, start + at, planes)] = some_bands[at]
        for at in range(0, half_planes, 2):
            z = plane_at(slots, start + at, planes) >> 1
            for c in range(coils):
                lines[c * slices + z] = some_lines[c * (slices // 2) + at // 2]
    found = readout_of(lines, readout)
    sums[...] = jnp.broadcast_to(jnp.sum(found * found), sums.shape)
    norm[...] = jnp.broadcast_to(jnp.sum(square), norm.shape)
    for c in range(coils):
        for z in range(slices):
            i = c * slices + z
            spectrum[c, :, z, :] = found[i * lp : i * lp + count]
    own = own_rows.shape[0]
    pairs = own_rows.shape[1] // 2
    for i in range(own):
        for plane in range(2):
            got = pairs_of(bands, (coil * own + i) * 2 + plane, pairs, tiles)
            turned = pltpu.roll(got, cols, 1)
            for r in range(pairs):
                own_rows[i, 2 * r, plane, :] = got[r, :cols]
                own_rows[i, 2 * r + 1, plane, :] = turned[r, :cols]


def last_body(totals, norm, image, own, residual, spectrum, image_out, residual_out):
    image_norm = jnp.sum(totals[:, :1])
    step = norm[:, :1] / (image_norm + 1e-06)
    image_out[...] = image[...] - step[0, 0] * own[...]
    residual_out[...] = residual[...] - step[0, 0] * spectrum[...]


def exchange_pairs(partner, shots, coils):
    pairs = []
    for s in range(shots):
        for c in range(coils):
            t, d = partner(s, c)
            pairs.append((s * coils + c, t * coils + d))
    return pairs


def slot_table(shots, coil_parts, planes):
    shot_bits, coil_bits = range(2, shots.bit_length() - 1), range(1, coil_parts.bit_length() - 1)
    table = []
    for shot in range(shots):
        for coil in range(coil_parts):
            ways = ((shot >> 1) & 1, coil & 1)
            a, b = (ways[1], ways[0]) if shot % 2 == 0 else ways
            row = [
                (shot & 1) * (planes // 2) + a * (planes // 4), b,
                (1 - (shot & 1)) * (planes // 2) + b * (planes // 4), a, shot, coil,
            ]
            for s in range(shots):
                for c in range(coil_parts):
                    ds, dc = s ^ shot, c ^ coil
                    rest = [(ds >> i) & 1 for i in shot_bits] + [(dc >> i) & 1 for i in coil_bits]
                    one, two = (ds >> 1) & 1, dc & 1
                    bits = rest[::-1] + ([one, two] if s % 2 == 0 else [two, one]) + [ds & 1]
                    row.append(sum(bit << i for i, bit in enumerate(bits)))
            table.append(row)
    return np.array(table, np.int32)


def shards(shots, coil_parts, image, sensitivity, warp_table, warp_source, warp_live, sampled_lines, measured):
    coils, slices, _, rows, cols = sensitivity.shape
    members, width = warp_table.shape[1], warp_table.shape[2]
    blocks = warp_source.shape[1]
    count = sampled_lines.shape[1]
    lp = round_up(count, 16)
    own_slices = image.shape[0]
    slab = blocks // shots
    planes = 2 * slices

    core = lambda s, c: (s ^ 1, c)
    by_shot = lambda s, c: (s ^ 2, c)
    by_coil = lambda s, c: (s, c ^ 1)
    first_way = lambda s, c: by_coil(s, c) if s & 1 == 0 else by_shot(s, c)
    second_way = lambda s, c: by_shot(s, c) if s & 1 == 0 else by_coil(s, c)
    rest = [lambda s, c, b=b: (s ^ b, c) for b in (1 << i for i in range(2, shots.bit_length() - 1))]
    rest += [lambda s, c, b=b: (s, c ^ b) for b in (1 << i for i in range(1, coil_parts.bit_length() - 1))]

    def swap(value, partner):
        return lax.ppermute(value, AXES, exchange_pairs(partner, shots, coil_parts))

    piece = image.astype(BF).reshape(1, own_slices * 2 * slab, width)
    for i in reversed(range(len(rest))):
        got = swap(piece, rest[i])
        piece = jnp.concatenate([piece, got], axis=0)
    second = swap(piece, second_way)
    early = swap(piece, first_way)
    late = swap(second, first_way)
    piece = jnp.concatenate([piece, second, early, late], axis=0)
    other = swap(piece, core)

    table = slot_table(shots, coil_parts, planes)
    slots = lax.dynamic_slice(
        jnp.asarray(table), (lax.axis_index(AXES), 0), (1, table.shape[1]), allow_negative_indices=False
    )[0]
    readout_np, lines_np = dft_tables(rows, cols)
    readout, line_tables = jnp.asarray(readout_np), jnp.asarray(lines_np)
    kernels = warp_table[0]
    shape = jax.ShapeDtypeStruct
    vmem = lambda value: pltpu.VMEM(value.shape, value.dtype)
    source, live = warp_source[0].T, warp_live[0].T
    both = [vmem(source), vmem(live)]
    sems = pltpu.SemaphoreType.DMA((2,))
    spread = call(
        spread_body, shape((blocks, members * blocks), BF), slices,
        scratch=both + [pltpu.VMEM((1, members * blocks), jnp.int32), sems], smem=1, far=2,
    )(slots, source, live)
    pick = call(
        pick_body, shape((members, blocks, blocks), BF), slices, scratch=both + [sems], smem=1, far=2,
    )(slots, source, live)
    seen = measured[0].transpose(0, 2, 1, 3)
    rows_first = image.transpose(0, 2, 1, 3)
    kept = [readout, kernels, seen, rows_first]
    maps = sensitivity.reshape(coils, 2 * slices, rows, cols)
    rows_table, cols_table, *refs = call(
        functools.partial(tables_body, coils=coils, kept=len(kept)),
        [shape((4 * lp, rows), BF), shape((rows, 4 * lp), BF)]
        + [shape((2 * slices, rows // 2, 2 * cols), BF)] * coils
        + [shape(value.shape, value.dtype) for value in kept],
        slices,
        scratch=[
            vmem(maps), vmem(sampled_lines), vmem(line_tables), pltpu.VMEM((1, 128), jnp.int32),
            pltpu.VMEM((-(-cols // width), rows, width), F32),
            pltpu.SemaphoreType.DMA((3 + len(kept),)),
        ],
        far=3 + len(kept),
    )(maps, sampled_lines, line_tables, *kept)
    sens, (readout, kernels, seen, rows_first) = refs[:coils], refs[coils:]
    sizes = dict(slab=slab, coils=coils)
    batch = coils * slices
    shaped = shape((planes // 2, 2, blocks // 2, width), BF)
    residual, send, rest_planes = call(
        functools.partial(first_body, slices=slices, shots=shots, coil_parts=coil_parts, **sizes),
        [shape(seen.shape, F32), shaped, shape((planes // 2, blocks, width), BF)],
        slices,
        scratch=[
            pltpu.VMEM((shots * coil_parts,) + piece.shape[1:], BF),
            pltpu.VMEM((slices, blocks, 2 * width), F32),
            pltpu.VMEM((planes, blocks, width), F32),
            pltpu.VMEM((batch, lp, 2 * cols), BF),
        ],
        smem=1,
    )(slots, piece, other, pick, spread, kernels, *sens, rows_table, cols_table, readout, seen)
    got = swap(send, core)
    keep = call(keep_body, shaped, slices, smem=1)(slots, rest_planes, spread, kernels)

    def add(left, right):
        return (left.astype(F32) + right.astype(F32)).astype(BF)

    quarter = planes // 4
    out2, stay2 = add(keep[quarter:], got[quarter:]), add(keep[:quarter], got[:quarter])
    got = swap(out2[:, 1], first_way)
    stay_got = swap(out2[:, 0], first_way)
    out3, total = add(stay2[:, 1], got), add(stay2[:, 0], stay_got)
    got = swap(out3, second_way)
    total = add(total, got)
    for partner in rest:
        total = add(total, swap(total, partner))
    second = swap(total, second_way)
    early = swap(total, first_way)
    late = swap(second, first_way)
    near = jnp.concatenate(
        [jnp.stack([total, second], axis=1), jnp.stack([early, late], axis=1)], axis=0
    )
    far = swap(near, core)

    devices = shots * coil_parts
    slab_rows = round_up(slab, 16)
    work = [pltpu.VMEM((blocks, 2 * width), BF), pltpu.VMEM((2, blocks, width), F32)]
    lines_half, bands_half = (batch // 2, lp, 2 * cols), (planes // 2, slab_rows, width)
    near_lines, near_bands, near_square = call(
        functools.partial(near_body, **sizes),
        [shape(lines_half, BF), shape(bands_half, F32), shape((8, 2 * width), F32)],
        slices, scratch=work, smem=1,
    )(slots, near, pick, kernels, *sens, rows_table)
    spectrum, sums, norm, own = call(
        functools.partial(second_body, **sizes),
        [
            shape(seen.shape, F32),
            shape((devices, 128), F32),
            shape((1, 128), F32),
            shape((own_slices, image.shape[2], 2, cols), F32),
        ],
        slices,
        scratch=work
        + [
            pltpu.VMEM(lines_half, BF),
            pltpu.VMEM(bands_half, F32),
            pltpu.VMEM((batch, lp, 2 * cols), BF),
            pltpu.VMEM((planes, slab_rows, width), F32),
        ],
        smem=1,
    )(slots, far, near_lines, near_bands, near_square, pick, kernels, *sens, rows_table, readout)
    totals = lax.all_to_all(sums, AXES, 0, 0, tiled=True)
    image, residual = call(
        last_body, [shape(rows_first.shape, F32), shape(seen.shape, F32)], slices
    )(totals, norm, rows_first, own, residual, spectrum)
    return image.transpose(0, 2, 1, 3), residual.transpose(0, 2, 1, 3)[None]


def solution(mesh):
    def body(*args):
        return shards(mesh.shape["shot"], mesh.shape["coil"], *args)

    return jax.shard_map(
        body,
        mesh=mesh,
        in_specs=(
            P("coil", None, "shot", None),
            P("coil", None, None, None, None),
            P("shot", None, None, None),
            P("shot", None, None),
            P("shot", None, None),
            P("shot", None),
            P("shot", "coil", None, None, None),
        ),
        out_specs=(P("coil", None, "shot", None), P("shot", "coil", None, None, None)),
        check_vma=False,
    )
```

```python
import functools
import math

import jax
import jax.numpy as jnp
import numpy as np
from jax import lax
from jax.experimental import pallas as pl
from jax.experimental.pallas import tpu as pltpu
from jax.sharding import PartitionSpec as P


BF = jnp.bfloat16
F32 = jnp.float32
AXES = ("shot", "coil")


def round_up(value, unit):
    return -(-value // unit) * unit


def dft_tables(rows, cols):
    def parts(length):
        index = np.arange(length, dtype=np.int64)
        angle = (index[:, None] * index[None, :] % length) * (-2.0 * math.pi / length)
        return np.cos(angle) / math.sqrt(length), np.sin(angle) / math.sqrt(length)

    real, imag = parts(cols)
    readout = np.block([[real, imag], [-imag, real]])
    real, imag = parts(rows)
    lines = []
    for odd in (0, 1):
        re, im = real[:, odd::2], imag[:, odd::2]
        lines.append(np.concatenate([re, -im], axis=1).T)
        lines.append(np.concatenate([im, re], axis=1).T)
    as_bf = lambda t: t.astype(np.float32).astype(jnp.bfloat16)
    return as_bf(readout), as_bf(np.stack(lines))


def dot(left, right):
    return jnp.dot(left, right, preferred_element_type=F32)


def dot_nt(left, right):
    return lax.dot_general(left, right, (((1,), (1,)), ((), ())), preferred_element_type=F32)


def call(body, out_shape, slices, scratch=(), smem=0, far=0):
    def run(*args):
        near = len(args) - smem - far
        specs = [pl.BlockSpec(memory_space=pltpu.SMEM)] * smem
        specs += [pl.BlockSpec(memory_space=pltpu.VMEM)] * near
        specs += [pl.BlockSpec(memory_space=pl.ANY)] * far
        args = list(args[: smem + near]) + [
            pltpu.with_memory_space_constraint(arg, pltpu.HBM) for arg in args[smem + near :]
        ]
        return pl.pallas_call(
            body,
            out_shape=out_shape,
            in_specs=specs,
            out_specs=jax.tree.map(lambda _: pl.BlockSpec(memory_space=pltpu.VMEM), out_shape),
            scratch_shapes=list(scratch),
            compiler_params=pltpu.CompilerParams(
                vmem_limit_bytes=min(8 + 6 * slices, 56) * 1024 * 1024
            ),
        )(*args)

    return run


def fetch(pairs, sems):
    copies = [pltpu.make_async_copy(a, b, sems.at[i]) for i, (a, b) in enumerate(pairs)]
    for copy in copies:
        copy.start()
    return copies


def spread_body(wanted, spread):
    down = lax.broadcasted_iota(jnp.int32, spread.shape, 0)
    spread[...] = jnp.where(down == jnp.broadcast_to(wanted[...], spread.shape), 1.0, 0.0).astype(BF)


def pick_body(slots, source_far, live_far, pick, wanted, source, live, sems):
    members, blocks, _ = pick.shape
    for copy in fetch([(source_far, source), (live_far, live)], sems):
        copy.wait()
    table = jnp.where(live[...] != 0, source[...], -1)
    full = round_up(blocks, 128)
    along = lax.broadcasted_iota(jnp.int32, (blocks, blocks), 1).astype(F32)
    for k in range(members):
        by_col = table[k : k + 1, :]
        wanted[:, k * blocks : (k + 1) * blocks] = by_col
        flat = jnp.broadcast_to(by_col, (8, blocks)).astype(F32)
        if full > blocks:
            flat = jnp.concatenate([flat, jnp.zeros((8, full - blocks), F32)], axis=1)
        by_row = flat.T[:blocks, :1]
        pick[k] = jnp.where(along == by_row, 1.0, 0.0).astype(BF)


def tables_body(*refs, coils, kept):
    maps_far, lines_far, line_tables_far, *refs = refs
    kept_far, refs = refs[:kept], refs[kept:]
    rows_out, cols_out, *refs = refs
    sens, kept_out, refs = refs[:coils], refs[coils : coils + kept], refs[coils + kept :]
    maps, lines, line_tables, padded, wide, sems = refs
    first, second, third, *rest = fetch(
        [(maps_far, maps), (line_tables_far, line_tables), (lines_far, lines), *zip(kept_far, kept_out)],
        sems,
    )
    first.wait()
    for c in range(coils):
        pair_body(maps, c, sens[c], wide)
    second.wait()
    third.wait()
    lines_body(lines, line_tables, rows_out, cols_out, padded)
    for copy in rest:
        copy.wait()


def lines_body(lines, tables, rows_out, cols_out, padded):
    lp = rows_out.shape[0] // 4
    count = tables.shape[2]
    padded[...] = jnp.full(padded.shape, -1, jnp.int32)
    padded[:, : lines.shape[1]] = lines[...]
    wide = jnp.broadcast_to(padded[:, :lp], (count, lp))
    chosen = jnp.where(lax.broadcasted_iota(jnp.int32, (count, lp), 0) == wide, 1.0, 0.0).astype(BF)
    eye = lax.broadcasted_iota(jnp.int32, (lp, lp), 0) == lax.broadcasted_iota(jnp.int32, (lp, lp), 1)
    eye = jnp.where(eye, 1.0, 0.0).astype(BF)
    for part in range(4):
        got = dot(tables[part], chosen).astype(BF)
        cols_out[:, part * lp : (part + 1) * lp] = got
        rows_out[part * lp : (part + 1) * lp, :] = dot_nt(eye, got).astype(BF)


def pair_body(maps, coil, out, wide):
    count, rows, cols = maps.shape[1:]
    half = rows // 2
    low = lax.broadcasted_iota(jnp.int32, (half, 2 * cols), 1) < cols
    width = wide.shape[2]
    used = range(0, cols, width)
    spare = [jnp.zeros((half, 2 * cols - width * len(used)), F32)]
    for i in range(count):
        for t, start in enumerate(used):
            stop = min(start + width, cols)
            wide[t, :, : stop - start] = maps[coil, i, :, start:stop].astype(F32)
        even, odd = (
            jnp.concatenate([wide[t, pl.ds(e, half, stride=2), :] for t in range(len(used))] + spare, axis=1)
            for e in range(2)
        )
        out[i] = jnp.where(low, even, pltpu.roll(odd, cols, 1)).astype(BF)


def halves_dot(left, right):
    half = left.shape[0] // 2
    return jnp.concatenate([dot(left[:half, :], right), dot(left[half:, :], right)], axis=0)


def warp(volume, pick, kernels, width):
    members = kernels.shape[0]
    picked = [dot(pick[k], volume).astype(BF) for k in range(members)]
    table = jnp.concatenate([kernels[k] for k in range(members)], axis=0)
    planes = []
    for e in range(2):
        cut = slice(e * width, (e + 1) * width)
        planes.append(dot(jnp.concatenate([p[:, cut] for p in picked], axis=1), table))
    return jnp.concatenate(planes, axis=1)


def unwarp(planes, spread, kernels):
    members = kernels.shape[0]
    rows = [
        jnp.concatenate([dot_nt(plane, kernels[k]) for plane in planes], axis=1).astype(BF)
        for k in range(members)
    ]
    return halves_dot(spread, jnp.concatenate(rows, axis=0)).astype(BF)


def pairs_of(ref, plane, rows, tiles):
    return jnp.concatenate([ref[plane, pl.ds(j, rows, stride=tiles), :] for j in range(tiles)], axis=1)


def coil_rows(warped, at, sens, z, rows_table, place, lines):
    width = warped.shape[2]
    half, wide = sens[0].shape[1], sens[0].shape[2]
    cols = wide // 2
    tiles = wide // width
    lp = rows_table.shape[0] // 4
    real = pairs_of(warped, at, half, tiles).astype(BF)
    imag = pairs_of(warped, at + 1, half, tiles).astype(BF)
    low = lax.broadcasted_iota(jnp.int32, (lp, wide), 1) < cols
    for c, maps in enumerate(sens):
        sr, si = maps[2 * z], maps[2 * z + 1]
        coil = jnp.concatenate([sr * real - si * imag, sr * imag + si * real], axis=0)
        found = dot(rows_table[...], coil)
        stay = jnp.where(low, found[:lp], found[3 * lp :])
        move = jnp.where(low, found[lp : 2 * lp], found[2 * lp : 3 * lp])
        lines[place(c)] = (stay + pltpu.roll(move, cols, 1)).astype(BF)


def readout_of(lines, readout):
    batch, lp, wide = lines.shape
    return dot(lines[...].reshape(batch * lp, wide), readout[...])


def plane_at(slots, position, planes):
    half = planes // 2
    return position ^ slots[0] if position < half else (position - half) ^ slots[2]


def put_halves(target, at, turn, planes):
    rows, width = planes.shape[0] // 2, planes.shape[1] // 2
    for e in range(2):
        for h in range(2):
            target[at + e, h ^ turn] = planes[h * rows : (h + 1) * rows, e * width : (e + 1) * width]


def first_body(slots, mine, other, pick, spread, kernels, *refs, slab, coils, slices, shots, coil_parts):
    sens, refs = refs[:coils], refs[coils:]
    rows_table, cols_table, readout, measured, residual, send, rest, pieces, volume, warped, lines = refs
    width = warped.shape[2]
    half, wide = sens[0].shape[1], sens[0].shape[2]
    cols = wide // 2
    tiles = wide // width
    lp = rows_table.shape[0] // 4
    count = measured.shape[1]
    per_part = slices // coil_parts
    own = mine.shape[0]
    pieces[:own] = mine[...]
    pieces[own:] = other[...]
    for z in range(slices):
        part, inner = z // per_part, z % per_part
        for s in range(shots):
            piece = pieces[slots[6 + s * coil_parts + part]].astype(F32)
            for plane in range(2):
                start = (inner * 2 + plane) * slab
                volume[z, s * slab : (s + 1) * slab, plane * width : (plane + 1) * width] = piece[
                    start : start + slab
                ]
        moved = warp(volume[z].astype(BF), pick, kernels, width)
        for plane in range(2):
            moved_plane = moved[:, plane * width : (plane + 1) * width]
            warped[2 * z + plane] = moved_plane.astype(BF).astype(F32)
        coil_rows(warped, 2 * z, sens, z, rows_table, lambda c, z=z: c * slices + z, lines)
    spectrum = readout_of(lines, readout)
    for c in range(coils):
        for z in range(slices):
            i = c * slices + z
            left = spectrum[i * lp : i * lp + count] - measured[c, :, z, :]
            residual[c, :, z, :] = left
            if count < lp:
                left = jnp.concatenate([left, jnp.zeros((lp - count, wide), F32)], axis=0)
            lines[i] = left.astype(BF)
    back = dot_nt(lines[...].reshape(coils * slices * lp, wide), readout[...])
    low = lax.broadcasted_iota(jnp.int32, (lp, wide), 1) < cols
    zero = jnp.zeros((lp, wide), F32)
    for z in range(slices):
        real, imag = None, None
        for c in range(coils):
            i = c * slices + z
            rows = back[i * lp : (i + 1) * lp]
            turned = pltpu.roll(rows, cols, 1)
            spreadout = jnp.concatenate(
                [
                    jnp.where(low, rows, zero),
                    jnp.where(low, turned, zero),
                    jnp.where(low, zero, turned),
                    jnp.where(low, zero, rows),
                ],
                axis=0,
            ).astype(BF)
            got = dot(cols_table[...], spreadout).astype(BF)
            gr, gi = got[:half], got[half:]
            sr, si = sens[c][2 * z], sens[c][2 * z + 1]
            more_real, more_imag = sr * gr + si * gi, sr * gi - si * gr
            real = more_real if real is None else real + more_real
            imag = more_imag if imag is None else imag + more_imag
        for j in range(tiles):
            cut = slice(j * width, (j + 1) * width)
            warped[2 * z, pl.ds(j, half, stride=tiles), :] = real[:, cut].astype(F32)
            warped[2 * z + 1, pl.ds(j, half, stride=tiles), :] = imag[:, cut].astype(F32)
    planes = 2 * slices
    for at in range(0, planes // 2, 2):
        chosen = [warped[plane_at(slots, planes // 2 + at + e, planes)].astype(BF) for e in range(2)]
        put_halves(send, at, slots[3], unwarp(chosen, spread, kernels))
    for at in range(planes // 2):
        rest[at] = warped[plane_at(slots, at, planes)].astype(BF)


def keep_body(slots, rest, spread, kernels, keep):
    for at in range(0, rest.shape[0], 2):
        put_halves(keep, at, slots[1], unwarp([rest[at], rest[at + 1]], spread, kernels))


def forward_part(slots, start, source, pick, kernels, sens, rows_table, lines, bands, volume, warped, *, slab):
    half_planes = source.shape[0]
    planes = 2 * half_planes
    blocks, width = warped.shape[1], warped.shape[2]
    rows = blocks // 2
    turn = slots[1] if start == 0 else slots[3]
    slab_rows = bands.shape[1]
    at_row = lax.broadcasted_iota(jnp.int32, (slab_rows, blocks), 0) + slots[4] * slab
    mine = jnp.where(lax.broadcasted_iota(jnp.int32, (slab_rows, blocks), 1) == at_row, 1.0, 0.0).astype(BF)
    square = jnp.zeros((8, 2 * width), F32)
    for at in range(0, half_planes, 2):
        for e in range(2):
            for h in range(2):
                volume[h * rows : (h + 1) * rows, e * width : (e + 1) * width] = source[at + e, h ^ turn]
        value = volume[...]
        as_f32 = value.astype(F32)
        square = square + jnp.sum((as_f32 * as_f32).reshape(blocks // 8, 8, 2 * width), axis=0)
        band = dot(mine, value)
        moved = warp(value, pick, kernels, width)
        for e in range(2):
            plane = plane_at(slots, start + at + e, planes)
            cut = slice(e * width, (e + 1) * width)
            warped[plane & 1] = moved[:, cut].astype(BF).astype(F32)
            bands[at + e] = band[:, cut]
        z = plane_at(slots, start + at, planes) >> 1
        coil_rows(warped, 0, sens, z, rows_table, lambda c, at=at: c * (half_planes // 2) + at // 2, lines)
    return square


def near_body(slots, near, pick, kernels, *refs, slab, coils):
    sens, refs = refs[:coils], refs[coils:]
    rows_table, lines, bands, square, volume, warped = refs
    square[...] = forward_part(
        slots, 0, near, pick, kernels, sens, rows_table, lines, bands, volume, warped, slab=slab
    )


def second_body(slots, far, near_lines, near_bands, near_square, pick, kernels, *refs, slab, coils):
    sens, refs = refs[:coils], refs[coils:]
    rows_table, readout, spectrum, sums, norm, own_rows, *refs = refs
    volume, warped, far_lines, far_bands, lines, bands = refs
    half_planes = far.shape[0]
    planes = 2 * half_planes
    slices = half_planes
    width = warped.shape[2]
    wide = sens[0].shape[2]
    cols = wide // 2
    tiles = wide // width
    lp = rows_table.shape[0] // 4
    count = spectrum.shape[1]
    coil = slots[5]
    square = near_square[...] + forward_part(
        slots, half_planes, far, pick, kernels, sens, rows_table, far_lines, far_bands, volume, warped,
        slab=slab,
    )
    for start, some_lines, some_bands in ((0, near_lines, near_bands), (half_planes, far_lines, far_bands)):
        for at in range(half_planes):
            bands[plane_at(slots, start + at, planes)] = some_bands[at]
        for at in range(0, half_planes, 2):
            z = plane_at(slots, start + at, planes) >> 1
            for c in range(coils):
                lines[c * slices + z] = some_lines[c * (slices // 2) + at // 2]
    found = readout_of(lines, readout)
    sums[...] = jnp.broadcast_to(jnp.sum(found * found), sums.shape)
    norm[...] = jnp.broadcast_to(jnp.sum(square), norm.shape)
    for c in range(coils):
        for z in range(slices):
            i = c * slices + z
            spectrum[c, :, z, :] = found[i * lp : i * lp + count]
    own = own_rows.shape[0]
    pairs = own_rows.shape[1] // 2
    for i in range(own):
        for plane in range(2):
            got = pairs_of(bands, (coil * own + i) * 2 + plane, pairs, tiles)
            turned = pltpu.roll(got, cols, 1)
            for r in range(pairs):
                own_rows[i, 2 * r, plane, :] = got[r, :cols]
                own_rows[i, 2 * r + 1, plane, :] = turned[r, :cols]


def last_body(totals, norm, image, own, residual, spectrum, image_out, residual_out):
    image_norm = jnp.sum(totals[:, :1])
    step = norm[:, :1] / (image_norm + 1e-06)
    image_out[...] = image[...] - step[0, 0] * own[...]
    residual_out[...] = residual[...] - step[0, 0] * spectrum[...]


def exchange_pairs(partner, shots, coils):
    pairs = []
    for s in range(shots):
        for c in range(coils):
            t, d = partner(s, c)
            pairs.append((s * coils + c, t * coils + d))
    return pairs


def slot_table(shots, coil_parts, planes):
    shot_bits, coil_bits = range(2, shots.bit_length() - 1), range(1, coil_parts.bit_length() - 1)
    table = []
    for shot in range(shots):
        for coil in range(coil_parts):
            ways = ((shot >> 1) & 1, coil & 1)
            a, b = (ways[1], ways[0]) if shot % 2 == 0 else ways
            row = [
                (shot & 1) * (planes // 2) + a * (planes // 4), b,
                (1 - (shot & 1)) * (planes // 2) + b * (planes // 4), a, shot, coil,
            ]
            for s in range(shots):
                for c in range(coil_parts):
                    ds, dc = s ^ shot, c ^ coil
                    rest = [(ds >> i) & 1 for i in shot_bits] + [(dc >> i) & 1 for i in coil_bits]
                    one, two = (ds >> 1) & 1, dc & 1
                    bits = rest[::-1] + ([one, two] if s % 2 == 0 else [two, one]) + [ds & 1]
                    row.append(sum(bit << i for i, bit in enumerate(bits)))
            table.append(row)
    return np.array(table, np.int32)


def shards(shots, coil_parts, image, sensitivity, warp_table, warp_source, warp_live, sampled_lines, measured):
    coils, slices, _, rows, cols = sensitivity.shape
    members, width = warp_table.shape[1], warp_table.shape[2]
    blocks = warp_source.shape[1]
    count = sampled_lines.shape[1]
    lp = round_up(count, 16)
    own_slices = image.shape[0]
    slab = blocks // shots
    planes = 2 * slices

    core = lambda s, c: (s ^ 1, c)
    by_shot = lambda s, c: (s ^ 2, c)
    by_coil = lambda s, c: (s, c ^ 1)
    first_way = lambda s, c: by_coil(s, c) if s & 1 == 0 else by_shot(s, c)
    second_way = lambda s, c: by_shot(s, c) if s & 1 == 0 else by_coil(s, c)
    rest = [lambda s, c, b=b: (s ^ b, c) for b in (1 << i for i in range(2, shots.bit_length() - 1))]
    rest += [lambda s, c, b=b: (s, c ^ b) for b in (1 << i for i in range(1, coil_parts.bit_length() - 1))]

    def swap(value, partner):
        return lax.ppermute(value, AXES, exchange_pairs(partner, shots, coil_parts))

    piece = image.astype(BF).reshape(1, own_slices * 2 * slab, width)
    for i in reversed(range(len(rest))):
        got = swap(piece, rest[i])
        piece = jnp.concatenate([piece, got], axis=0)
    second = swap(piece, second_way)
    early = swap(piece, first_way)
    late = swap(second, first_way)
    piece = jnp.concatenate([piece, second, early, late], axis=0)
    other = swap(piece, core)

    table = slot_table(shots, coil_parts, planes)
    slots = lax.dynamic_slice(
        jnp.asarray(table), (lax.axis_index(AXES), 0), (1, table.shape[1]), allow_negative_indices=False
    )[0]
    readout_np, lines_np = dft_tables(rows, cols)
    readout, line_tables = jnp.asarray(readout_np), jnp.asarray(lines_np)
    kernels = warp_table[0]
    shape = jax.ShapeDtypeStruct
    vmem = lambda value: pltpu.VMEM(value.shape, value.dtype)
    source, live = warp_source[0].T, warp_live[0].T
    pick, wanted = call(
        pick_body,
        [shape((members, blocks, blocks), BF), shape((1, members * blocks), jnp.int32)],
        slices,
        scratch=[vmem(source), vmem(live), pltpu.SemaphoreType.DMA((2,))],
        smem=1,
        far=2,
    )(slots, source, live)
    spread = call(spread_body, shape((blocks, members * blocks), BF), slices)(wanted)
    seen = measured[0].transpose(0, 2, 1, 3)
    rows_first = image.transpose(0, 2, 1, 3)
    kept = [readout, kernels, seen, rows_first]
    maps = sensitivity.reshape(coils, 2 * slices, rows, cols)
    rows_table, cols_table, *refs = call(
        functools.partial(tables_body, coils=coils, kept=len(kept)),
        [shape((4 * lp, rows), BF), shape((rows, 4 * lp), BF)]
        + [shape((2 * slices, rows // 2, 2 * cols), BF)] * coils
        + [shape(value.shape, value.dtype) for value in kept],
        slices,
        scratch=[
            vmem(maps), vmem(sampled_lines), vmem(line_tables), pltpu.VMEM((1, 128), jnp.int32),
            pltpu.VMEM((-(-cols // width), rows, width), F32),
            pltpu.SemaphoreType.DMA((3 + len(kept),)),
        ],
        far=3 + len(kept),
    )(maps, sampled_lines, line_tables, *kept)
    sens, (readout, kernels, seen, rows_first) = refs[:coils], refs[coils:]
    sizes = dict(slab=slab, coils=coils)
    batch = coils * slices
    shaped = shape((planes // 2, 2, blocks // 2, width), BF)
    residual, send, rest_planes = call(
        functools.partial(first_body, slices=slices, shots=shots, coil_parts=coil_parts, **sizes),
        [shape(seen.shape, F32), shaped, shape((planes // 2, blocks, width), BF)],
        slices,
        scratch=[
            pltpu.VMEM((shots * coil_parts,) + piece.shape[1:], BF),
            pltpu.VMEM((slices, blocks, 2 * width), F32),
            pltpu.VMEM((planes, blocks, width), F32),
            pltpu.VMEM((batch, lp, 2 * cols), BF),
        ],
        smem=1,
    )(slots, piece, other, pick, spread, kernels, *sens, rows_table, cols_table, readout, seen)
    got = swap(send, core)
    keep = call(keep_body, shaped, slices, smem=1)(slots, rest_planes, spread, kernels)

    def add(left, right):
        return (left.astype(F32) + right.astype(F32)).astype(BF)

    quarter = planes // 4
    out2, stay2 = add(keep[quarter:], got[quarter:]), add(keep[:quarter], got[:quarter])
    got = swap(out2[:, 1], first_way)
    stay_got = swap(out2[:, 0], first_way)
    out3, total = add(stay2[:, 1], got), add(stay2[:, 0], stay_got)
    got = swap(out3, second_way)
    total = add(total, got)
    for partner in reversed(rest):
        total = add(total, swap(total, partner))
    second = swap(total, second_way)
    early = swap(total, first_way)
    late = swap(second, first_way)
    near = jnp.concatenate(
        [jnp.stack([total, second], axis=1), jnp.stack([early, late], axis=1)], axis=0
    )
    far = swap(near, core)

    devices = shots * coil_parts
    slab_rows = round_up(slab, 16)
    work = [pltpu.VMEM((blocks, 2 * width), BF), pltpu.VMEM((2, blocks, width), F32)]
    lines_half, bands_half = (batch // 2, lp, 2 * cols), (planes // 2, slab_rows, width)
    near_lines, near_bands, near_square = call(
        functools.partial(near_body, **sizes),
        [shape(lines_half, BF), shape(bands_half, F32), shape((8, 2 * width), F32)],
        slices, scratch=work, smem=1,
    )(slots, near, pick, kernels, *sens, rows_table)
    spectrum, sums, norm, own = call(
        functools.partial(second_body, **sizes),
        [
            shape(seen.shape, F32),
            shape((devices, 128), F32),
            shape((1, 128), F32),
            shape((own_slices, image.shape[2], 2, cols), F32),
        ],
        slices,
        scratch=work
        + [
            pltpu.VMEM(lines_half, BF),
            pltpu.VMEM(bands_half, F32),
            pltpu.VMEM((batch, lp, 2 * cols), BF),
            pltpu.VMEM((planes, slab_rows, width), F32),
        ],
        smem=1,
    )(slots, far, near_lines, near_bands, near_square, pick, kernels, *sens, rows_table, readout)
    totals = lax.all_to_all(sums, AXES, 0, 0, tiled=True)
    image, residual = call(
        last_body, [shape(rows_first.shape, F32), shape(seen.shape, F32)], slices
    )(totals, norm, rows_first, own, residual, spectrum)
    return image.transpose(0, 2, 1, 3), residual.transpose(0, 2, 1, 3)[None]


def solution(mesh):
    def body(*args):
        return shards(mesh.shape["shot"], mesh.shape["coil"], *args)

    return jax.shard_map(
        body,
        mesh=mesh,
        in_specs=(
            P("coil", None, "shot", None),
            P("coil", None, None, None, None),
            P("shot", None, None, None),
            P("shot", None, None),
            P("shot", None, None),
            P("shot", None),
            P("shot", "coil", None, None, None),
        ),
        out_specs=(P("coil", None, "shot", None), P("shot", "coil", None, None, None)),
        check_vma=False,
    )
```
